32 devices in a mesh: player: 2 (over x), feat: 16 (over z, y, core).
Axes of the slice: x: 2, y: 2, z: 4, core: 2. Of those that a mesh axis runs over, the one named last changes fastest.
Arguments:
- slab: bfloat16 [128, 524288], P(None, 'feat'), may hold values from -16 to 16
- players: bfloat16 [512, 524288], P('player', 'feat'), may hold values from -16 to 16
Outputs:
- updated: bfloat16 [512, 524288], P('player', 'feat')
The draws below stay inside these ranges and needn't reach their ends.
All inputs are finite; a program needn't handle non-finite values.
Results may differ from the reference program's by a relative error of at most 0.0083.
Values may be sent and summed in bfloat16 or wider, within the bound.
No kernel may reach another device: no remote copies, remote signals or barrier semaphores. Data moves between devices by JAX's collectives and lax.ppermute only.
A program may use at most 192 MiB of HBM per device.

```python
import math
import jax
import jax.numpy as jnp
from jax import lax

F = 524288
K = 512
B = 128
STEPS = 2


def slab_pair(key):
    base = jax.random.fold_in(key, 4242)
    key_slab = jax.random.fold_in(base, 0)
    key_mix = jax.random.fold_in(base, 1)
    key_noise = jax.random.fold_in(base, 2)
    key_freq = jax.random.fold_in(base, 5)
    key_phase = jax.random.fold_in(base, 6)
    unit_slab = jax.random.truncated_normal(key_slab, -4.0, 4.0, (B, F), jnp.float32)
    slab = jnp.clip(unit_slab, -16.0, 16.0)
    mixing = jax.random.normal(key_mix, (K, B), jnp.float32)
    span = 0.8 * jnp.dot(mixing, unit_slab) / math.sqrt(B)
    frequency = jax.random.uniform(key_freq, (K, 1), jnp.float32, 1.0, 3.0)
    phase = jax.random.uniform(key_phase, (K, 1), jnp.float32, 0.0, 1.0)
    position = jnp.arange(F, dtype=jnp.float32)[None, :] / F
    profile = 0.5 + 0.5 * jnp.sin(2.0 * math.pi * (frequency * position + phase))
    amplitude = jnp.exp(math.log(9.0) * (profile - 0.5))
    noise = 0.6 * jax.random.normal(key_noise, (K, F), jnp.float32) * amplitude
    players = jnp.clip(span + noise, -16.0, 16.0)
    return (slab, players)


def draw_slab(key, part):
    return slab_pair(key)[0].astype(jnp.bfloat16)


def draw_players(key, part):
    return slab_pair(key)[1].astype(jnp.bfloat16)


def setup_inputs(seed: int = 0) -> dict:
    splits = jax.random.split(jax.random.key(seed), 3)
    return {
        "slab": draw_slab(jax.random.fold_in(splits[2], 71), 0),
        "players": draw_players(jax.random.fold_in(splits[2], 71), 0),
    }


def reference(slab, players):
    block = min(64, K)
    count = K // block
    inverse_square = 1.0 / F / F
    weights = players
    rows = jnp.arange(K)[:, None]
    cols = jnp.arange(K)[None, :]
    for step in range(STEPS):
        proj = lax.dot_general(weights, slab, (((1,), (1,)), ((), ())), preferred_element_type=jnp.float32)
        scaled = (proj / F).astype(jnp.bfloat16)
        correlation = jnp.dot(proj, proj.T, precision=lax.Precision.HIGHEST) * inverse_square
        coeff = jnp.where(rows < cols, correlation, jnp.zeros_like(correlation)).astype(jnp.bfloat16)
        coeff_blocks = coeff.reshape(K, count, block).transpose(1, 0, 2)
        scaled_blocks = scaled.reshape(count, block, B)
        weight_blocks = weights.reshape(count, block, F)

        def one_block(items):
            own_rows, own_scaled, own_coeff = items
            reward = jnp.dot(own_scaled, slab, preferred_element_type=jnp.float32)
            penalty = lax.dot_general(own_coeff, weights, (((0,), (0,)), ((), ())), preferred_element_type=jnp.float32)
            update = own_rows.astype(jnp.float32) + reward - penalty
            total = lax.optimization_barrier(jnp.sum(update * update, axis=1))
            return (update * jnp.sqrt(F / (total + 1e-06))[:, None]).astype(jnp.bfloat16)
        weights = lax.map(one_block, (weight_blocks, scaled_blocks, coeff_blocks)).reshape(K, F)
    return weights
```

```python
import functools

import jax
import jax.numpy as jnp
from jax import lax
from jax.experimental import pallas as pl
from jax.experimental.pallas import tpu as pltpu
from jax.sharding import PartitionSpec as P


EARLY = (1, 3, 4, 8)
LATE = (2, 2, 4, 4, 2, 1, 1)
UNIT = 32
BLOCK = 1024


HIGH = lax.Precision.HIGHEST


def dot(a, b, contract=((1,), (0,)), precision=None):
    return lax.dot_general(
        a, b, (contract, ((), ())), precision=precision, preferred_element_type=jnp.float32
    )


def through_bf16(x):
    return x.astype(jnp.bfloat16).astype(jnp.float32)


def scatter_sum(x, axis):
    size = lax.axis_size(axis)
    me = lax.axis_index(axis)
    step = 1
    while step < size:
        half = x.shape[0] // 2
        low, high = x[:half], x[half:]
        upper = (me & step) != 0
        send = jnp.where(upper, low, high)
        keep = jnp.where(upper, high, low)
        got = lax.ppermute(send, axis, [(i, i ^ step) for i in range(size)])
        x = keep + got
        step = step * 2
    return x


def gather_back(x, axis):
    size = lax.axis_size(axis)
    me = lax.axis_index(axis)
    step = size // 2
    while step:
        got = lax.ppermute(x, axis, [(i, i ^ step) for i in range(size)])
        upper = (me & step) != 0
        x = jnp.concatenate([jnp.where(upper, got, x), jnp.where(upper, x, got)], axis=-2)
        step = step // 2
    return x


def coeff_kernel(rows, features, gram_ref, down_ref, across_ref, j0_ref, j1_ref, d0_ref, d1_ref):
    span = j0_ref.shape[0]
    batch = gram_ref.shape[0] - span
    rest = span - rows
    inverse_square = 1.0 / features / features
    rhs = ((1,), (1,))

    def coefficients(left, right, first):
        corr = dot(left, right, rhs, HIGH) * inverse_square
        down, across = down_ref[first:, :], across_ref[...]
        mixing = jnp.where(across < down, -through_bf16(corr), 0.0)
        mixing = jnp.where(across == down, 1.0, mixing)
        return through_bf16(left / features), mixing

    def scale(left, product):
        norm = jnp.maximum(jnp.sum(left * product, axis=1, keepdims=True), 0.0)
        return jnp.sqrt(features / (norm + 1e-06))

    proj = gram_ref[batch:, :batch]
    reward, mixing = coefficients(proj, proj, 0)
    j0 = jnp.concatenate([reward, mixing], axis=1)
    y0 = dot(j0, gram_ref[...], precision=HIGH)
    d0 = scale(j0, y0)
    j0_ref[...] = j0.astype(jnp.bfloat16)
    d0_ref[...] = d0
    proj1 = d0 * y0[:, :batch]
    reward, mixing = coefficients(proj1[rest:], proj1, rest)
    j1_ref[:, :batch] = reward.astype(jnp.bfloat16)
    j1_ref[:, batch:] = mixing.astype(jnp.bfloat16)
    joint = dot(mixing, d0 * j0, precision=HIGH)
    joint = jnp.concatenate([joint[:, :batch] + reward, joint[:, batch:]], axis=1)
    d1_ref[...] = scale(joint, dot(joint, gram_ref[...], precision=HIGH))


def coefficients_of(gram, order, rows, features):
    span = order.shape[0]
    size = gram.shape[0]
    return pl.pallas_call(
        functools.partial(coeff_kernel, rows, features),
        out_shape=[
            jax.ShapeDtypeStruct((span, size), jnp.bfloat16),
            jax.ShapeDtypeStruct((rows, size), jnp.bfloat16),
            jax.ShapeDtypeStruct((span, 1), jnp.float32),
            jax.ShapeDtypeStruct((rows, 1), jnp.float32),
        ],
        cost_estimate=pl.CostEstimate(
            flops=24 * size * size * span, bytes_accessed=8 * size * size, transcendentals=0
        ),
        name="coefficients_of",
    )(gram, order[:, None], order[None, :])


def update_kernel(others, base_ref, w_ref, x_ref, *refs):
    other_refs = refs[:others]
    j0_ref, j1_ref, d0_ref, d1_ref = refs[others : others + 4]
    out_ref, stack, scaled = refs[-3:]
    rows, batch = w_ref.shape[0], x_ref.shape[0]
    rest = others * rows
    split = batch + rest
    stack[:batch, :] = x_ref[...]
    scaled[:batch, :] = x_ref[...]
    for i in range(others):
        stack[batch + i * rows : batch + (i + 1) * rows, :] = other_refs[i][...]
    stack[split:, :] = w_ref[...]
    first = dot(j0_ref[:rest, :split], stack[:split, :])
    scaled[batch:split, :] = (first * d0_ref[:rest, :]).astype(jnp.bfloat16)
    own = dot(j0_ref[rest:, :], stack[...])
    scaled[split:, :] = (own * d0_ref[rest:, :]).astype(jnp.bfloat16)
    out_ref[...] = (dot(j1_ref[...], scaled[...]) * d1_ref[...]).astype(jnp.bfloat16)


def update_piece(base, weights, slab, others, coeffs, out, width, block):
    rows, batch = weights.shape[0], slab.shape[0]
    count = len(others)
    shift = lambda i, b: (0, b[0] + i)
    whole = lambda i, b: (0, 0)
    in_specs = [pl.BlockSpec((rows, block), shift), pl.BlockSpec((batch, block), shift)]
    in_specs += [pl.BlockSpec((rows, block), lambda i, b: (0, i))] * count
    in_specs += [pl.BlockSpec(c.shape, whole) for c in coeffs]
    operands = [weights, slab, *others, *coeffs]
    aliases = {}
    if out is not None:
        in_specs.append(pl.BlockSpec(memory_space=pl.ANY))
        operands.append(out)
        aliases = {len(operands): 0}
    total = rows * (count + 1)
    return pl.pallas_call(
        functools.partial(update_kernel, count),
        out_shape=jax.ShapeDtypeStruct(weights.shape, jnp.bfloat16),
        grid_spec=pltpu.PrefetchScalarGridSpec(
            num_scalar_prefetch=1,
            grid=(width // block,),
            in_specs=in_specs,
            out_specs=pl.BlockSpec((rows, block), shift),
            scratch_shapes=[
                pltpu.VMEM((total + batch, block), jnp.bfloat16),
                pltpu.VMEM((total + batch, block), jnp.bfloat16),
            ],
        ),
        input_output_aliases=aliases,
        compiler_params=pltpu.CompilerParams(dimension_semantics=("arbitrary",)),
        cost_estimate=pl.CostEstimate(
            flops=2 * width * (total + batch) * (total + rows),
            bytes_accessed=2 * width * (2 * rows + batch + count * rows),
            transcendentals=0,
        ),
        name="update_piece",
    )(base, *operands)


def compute(slab, players):
    rows, width = players.shape
    batch = slab.shape[0]
    n = lax.axis_size("player")
    me = lax.axis_index("player")
    features = width * lax.axis_size("feat")
    half, unit = width // 2, width // UNIT
    ring = [[(i, (i + s) % n) for i in range(n)] for s in range(n)]

    sent_at = [jnp.where(me + s < n, 0, half) for s in range(n)]
    got_at = [jnp.where(me - s >= 0, 0, half) for s in range(n)]

    def send(s, start, size):
        piece = lax.dynamic_slice(players, (0, start), (rows, size))
        return lax.ppermute(piece, "player", ring[s])

    early, late, place = [], [], 0
    for units in EARLY:
        size = units * unit
        early.append((place, size, [send(s, sent_at[s] + place, size) for s in range(1, n)]))
        place += size
    place = 0
    for units in LATE:
        size = units * unit
        late.append(
            (
                place,
                size,
                [send(s, half - sent_at[s] + place, size) for s in range(1, n)],
            )
        )
        place += size

    rhs = ((1,), (1,))
    own_gram = dot(players, players, rhs)
    own_proj = dot(players, slab, rhs)
    slab_gram = dot(slab, slab, rhs)
    cross = []
    for s in range(1, n):
        total = 0.0
        for place, size, got in early:
            mine = lax.dynamic_slice(players, (0, got_at[s] + place), (rows, size))
            total = total + dot(mine, got[s - 1], rhs)
        cross.append(total)

    if batch >= rows:
        flat = [slab_gram[i : i + rows] for i in range(0, batch, rows)]
    else:
        flat = [jnp.pad(slab_gram, ((0, rows - batch), (0, 0)))]
    payload = jnp.concatenate([own_gram, *cross, own_proj, *flat], axis=1)
    part = scatter_sum(payload, "feat")
    parts = [part] + [lax.ppermute(part, "player", ring[s]) for s in range(1, n)]
    full = gather_back(jnp.stack(parts), "feat")

    span = n * rows
    turn = [*range(1, n), 0]
    block_of = lambda t, u: full[t, :, ((u - t) % n) * rows : ((u - t) % n + 1) * rows]
    pair = lambda t, u: block_of(t, u) if t == u else block_of(t, u) + block_of(u, t).T
    proj = jnp.concatenate([full[t, :, span : span + batch] for t in turn], axis=0)
    tail = full[0, :, span + batch :]
    if batch >= rows:
        hmat = jnp.concatenate(
            [tail[:, i * batch : (i + 1) * batch] for i in range(batch // rows)], axis=0
        )
    else:
        hmat = tail[:batch]
    lines = [jnp.concatenate([hmat, proj.T], axis=1)]
    for k, t in enumerate(turn):
        left = proj[k * rows : (k + 1) * rows]
        lines.append(jnp.concatenate([left, *[pair(t, u) for u in turn]], axis=1))
    gram = jnp.concatenate(lines, axis=0)
    order = jnp.concatenate(
        [((me - t) % n) * rows + jnp.arange(rows, dtype=jnp.int32) for t in turn]
    )
    coeffs = coefficients_of(gram, order, rows, features)

    block = min(BLOCK, unit)
    first = jnp.where(me > 0, 0, half)
    out = None
    for start, pieces in ((first, early), (half - first, late)):
        for place, size, got in pieces:
            base = ((start + place) // block).reshape(1).astype(jnp.int32)
            out = update_piece(base, players, slab, got, coeffs, out, size, block)
    return out


def solution(mesh):
    in_specs = (P(None, "feat"), P("player", "feat"))
    out_specs = P("player", "feat")
    return jax.shard_map(
        compute, mesh=mesh, in_specs=in_specs, out_specs=out_specs, check_vma=False
    )
```

```python
import functools

import jax
import jax.numpy as jnp
from jax import lax
from jax.experimental import pallas as pl
from jax.experimental.pallas import tpu as pltpu
from jax.sharding import PartitionSpec as P


EARLY = (1, 3, 8, 4)
LATE = (2, 2, 4, 4, 2, 1, 1)
UNIT = 32
BLOCK = 1024


HIGH = lax.Precision.HIGHEST


def dot(a, b, contract=((1,), (0,)), precision=None):
    return lax.dot_general(
        a, b, (contract, ((), ())), precision=precision, preferred_element_type=jnp.float32
    )


def through_bf16(x):
    return x.astype(jnp.bfloat16).astype(jnp.float32)


def scatter_sum(x, axis):
    size = lax.axis_size(axis)
    me = lax.axis_index(axis)
    step = 1
    while step < size:
        half = x.shape[0] // 2
        low, high = x[:half], x[half:]
        upper = (me & step) != 0
        send = jnp.where(upper, low, high)
        keep = jnp.where(upper, high, low)
        got = lax.ppermute(send, axis, [(i, i ^ step) for i in range(size)])
        x = keep + got
        step = step * 2
    return x


def gather_back(x, axis):
    size = lax.axis_size(axis)
    me = lax.axis_index(axis)
    step = size // 2
    while step:
        got = lax.ppermute(x, axis, [(i, i ^ step) for i in range(size)])
        upper = (me & step) != 0
        x = jnp.concatenate([jnp.where(upper, got, x), jnp.where(upper, x, got)], axis=-2)
        step = step // 2
    return x


def coeff_kernel(rows, features, gram_ref, down_ref, across_ref, j0_ref, j1_ref, d0_ref, d1_ref):
    span = j0_ref.shape[0]
    batch = gram_ref.shape[0] - span
    rest = span - rows
    inverse_square = 1.0 / features / features
    rhs = ((1,), (1,))

    def coefficients(left, right, first):
        corr = dot(left, right, rhs, HIGH) * inverse_square
        down, across = down_ref[first:, :], across_ref[...]
        mixing = jnp.where(across < down, -through_bf16(corr), 0.0)
        mixing = jnp.where(across == down, 1.0, mixing)
        return through_bf16(left / features), mixing

    def scale(left, product):
        norm = jnp.maximum(jnp.sum(left * product, axis=1, keepdims=True), 0.0)
        return jnp.sqrt(features / (norm + 1e-06))

    proj = gram_ref[batch:, :batch]
    reward, mixing = coefficients(proj, proj, 0)
    j0 = jnp.concatenate([reward, mixing], axis=1)
    y0 = dot(j0, gram_ref[...], precision=HIGH)
    d0 = scale(j0, y0)
    j0_ref[...] = j0.astype(jnp.bfloat16)
    d0_ref[...] = d0
    proj1 = d0 * y0[:, :batch]
    reward, mixing = coefficients(proj1[rest:], proj1, rest)
    j1_ref[:, :batch] = reward.astype(jnp.bfloat16)
    j1_ref[:, batch:] = mixing.astype(jnp.bfloat16)
    joint = dot(mixing, d0 * j0, precision=HIGH)
    joint = jnp.concatenate([joint[:, :batch] + reward, joint[:, batch:]], axis=1)
    d1_ref[...] = scale(joint, dot(joint, gram_ref[...], precision=HIGH))


def coefficients_of(gram, order, rows, features):
    span = order.shape[0]
    size = gram.shape[0]
    return pl.pallas_call(
        functools.partial(coeff_kernel, rows, features),
        out_shape=[
            jax.ShapeDtypeStruct((span, size), jnp.bfloat16),
            jax.ShapeDtypeStruct((rows, size), jnp.bfloat16),
            jax.ShapeDtypeStruct((span, 1), jnp.float32),
            jax.ShapeDtypeStruct((rows, 1), jnp.float32),
        ],
        cost_estimate=pl.CostEstimate(
            flops=24 * size * size * span, bytes_accessed=8 * size * size, transcendentals=0
        ),
        name="coefficients_of",
    )(gram, order[:, None], order[None, :])


def update_kernel(others, base_ref, w_ref, x_ref, *refs):
    other_refs = refs[:others]
    j0_ref, j1_ref, d0_ref, d1_ref = refs[others : others + 4]
    out_ref, stack, scaled = refs[-3:]
    rows, batch = w_ref.shape[0], x_ref.shape[0]
    rest = others * rows
    split = batch + rest
    stack[:batch, :] = x_ref[...]
    scaled[:batch, :] = x_ref[...]
    for i in range(others):
        stack[batch + i * rows : batch + (i + 1) * rows, :] = other_refs[i][...]
    stack[split:, :] = w_ref[...]
    first = dot(j0_ref[:rest, :split], stack[:split, :])
    scaled[batch:split, :] = (first * d0_ref[:rest, :]).astype(jnp.bfloat16)
    own = dot(j0_ref[rest:, :], stack[...])
    scaled[split:, :] = (own * d0_ref[rest:, :]).astype(jnp.bfloat16)
    out_ref[...] = (dot(j1_ref[...], scaled[...]) * d1_ref[...]).astype(jnp.bfloat16)


def update_piece(base, weights, slab, others, coeffs, out, width, block):
    rows, batch = weights.shape[0], slab.shape[0]
    count = len(others)
    shift = lambda i, b: (0, b[0] + i)
    whole = lambda i, b: (0, 0)
    in_specs = [pl.BlockSpec((rows, block), shift), pl.BlockSpec((batch, block), shift)]
    in_specs += [pl.BlockSpec((rows, block), lambda i, b: (0, i))] * count
    in_specs += [pl.BlockSpec(c.shape, whole) for c in coeffs]
    operands = [weights, slab, *others, *coeffs]
    aliases = {}
    if out is not None:
        in_specs.append(pl.BlockSpec(memory_space=pl.ANY))
        operands.append(out)
        aliases = {len(operands): 0}
    total = rows * (count + 1)
    return pl.pallas_call(
        functools.partial(update_kernel, count),
        out_shape=jax.ShapeDtypeStruct(weights.shape, jnp.bfloat16),
        grid_spec=pltpu.PrefetchScalarGridSpec(
            num_scalar_prefetch=1,
            grid=(width // block,),
            in_specs=in_specs,
            out_specs=pl.BlockSpec((rows, block), shift),
            scratch_shapes=[
                pltpu.VMEM((total + batch, block), jnp.bfloat16),
                pltpu.VMEM((total + batch, block), jnp.bfloat16),
            ],
        ),
        input_output_aliases=aliases,
        compiler_params=pltpu.CompilerParams(dimension_semantics=("arbitrary",)),
        cost_estimate=pl.CostEstimate(
            flops=2 * width * (total + batch) * (total + rows),
            bytes_accessed=2 * width * (2 * rows + batch + count * rows),
            transcendentals=0,
        ),
        name="update_piece",
    )(base, *operands)


def compute(slab, players):
    rows, width = players.shape
    batch = slab.shape[0]
    n = lax.axis_size("player")
    me = lax.axis_index("player")
    features = width * lax.axis_size("feat")
    half, unit = width // 2, width // UNIT
    ring = [[(i, (i + s) % n) for i in range(n)] for s in range(n)]

    sent_at = [jnp.where(me + s < n, 0, half) for s in range(n)]
    got_at = [jnp.where(me - s >= 0, 0, half) for s in range(n)]

    source = players

    def send(s, start, size):
        nonlocal source
        piece = lax.dynamic_slice(source, (0, start), (rows, size))
        source, piece = lax.optimization_barrier((source, piece))
        return lax.ppermute(piece, "player", ring[s])

    early, late, place = [], [], 0
    for units in EARLY:
        size = units * unit
        early.append((place, size, [send(s, sent_at[s] + place, size) for s in range(1, n)]))
        place += size
    place = 0
    for units in LATE:
        size = units * unit
        late.append(
            (
                place,
                size,
                [send(s, half - sent_at[s] + place, size) for s in range(1, n)],
            )
        )
        place += size

    rhs = ((1,), (1,))
    own_gram = dot(source, source, rhs)
    own_proj = dot(source, slab, rhs)
    slab_gram = dot(slab, slab, rhs)
    cross = []
    for s in range(1, n):
        total = 0.0
        for place, size, got in early:
            mine = lax.dynamic_slice(players, (0, got_at[s] + place), (rows, size))
            piece = got[s - 1]
            if place:
                total, piece = lax.optimization_barrier((total, piece))
            total = total + dot(mine, piece, rhs)
        cross.append(total)

    if batch >= rows:
        flat = [slab_gram[i : i + rows] for i in range(0, batch, rows)]
    else:
        flat = [jnp.pad(slab_gram, ((0, rows - batch), (0, 0)))]
    payload = jnp.concatenate([own_gram, *cross, own_proj, *flat], axis=1)
    part = scatter_sum(payload, "feat")
    parts = [part] + [lax.ppermute(part, "player", ring[s]) for s in range(1, n)]
    full = gather_back(jnp.stack(parts), "feat")

    span = n * rows
    turn = [*range(1, n), 0]
    block_of = lambda t, u: full[t, :, ((u - t) % n) * rows : ((u - t) % n + 1) * rows]
    pair = lambda t, u: block_of(t, u) if t == u else block_of(t, u) + block_of(u, t).T
    proj = jnp.concatenate([full[t, :, span : span + batch] for t in turn], axis=0)
    tail = full[0, :, span + batch :]
    if batch >= rows:
        hmat = jnp.concatenate(
            [tail[:, i * batch : (i + 1) * batch] for i in range(batch // rows)], axis=0
        )
    else:
        hmat = tail[:batch]
    lines = [jnp.concatenate([hmat, proj.T], axis=1)]
    for k, t in enumerate(turn):
        left = proj[k * rows : (k + 1) * rows]
        lines.append(jnp.concatenate([left, *[pair(t, u) for u in turn]], axis=1))
    gram = jnp.concatenate(lines, axis=0)
    order = jnp.concatenate(
        [((me - t) % n) * rows + jnp.arange(rows, dtype=jnp.int32) for t in turn]
    )
    coeffs = coefficients_of(gram, order, rows, features)

    block = min(BLOCK, unit)
    first = jnp.where(me > 0, 0, half)
    out = None
    for start, pieces in ((first, early), (half - first, late)):
        for place, size, got in pieces:
            base = ((start + place) // block).reshape(1).astype(jnp.int32)
            out = update_piece(base, players, slab, got, coeffs, out, size, block)
    return out


def solution(mesh):
    in_specs = (P(None, "feat"), P("player", "feat"))
    out_specs = P("player", "feat")
    return jax.shard_map(
        compute, mesh=mesh, in_specs=in_specs, out_specs=out_specs, check_vma=False
    )
```

```python
import functools

import jax
import jax.numpy as jnp
from jax import lax
from jax.experimental import pallas as pl
from jax.experimental.pallas import tpu as pltpu
from jax.sharding import PartitionSpec as P


EARLY = (1, 7, 16, 8)
LATE = (4, 4, 8, 8, 4, 2, 1, 1)
UNIT = 64
BLOCK = 1024


HIGH = lax.Precision.HIGHEST


def dot(a, b, contract=((1,), (0,)), precision=None):
    return lax.dot_general(
        a, b, (contract, ((), ())), precision=precision, preferred_element_type=jnp.float32
    )


def through_bf16(x):
    return x.astype(jnp.bfloat16).astype(jnp.float32)


def scatter_sum(x, axis):
    size = lax.axis_size(axis)
    me = lax.axis_index(axis)
    step = 1
    while step < size:
        half = x.shape[0] // 2
        low, high = x[:half], x[half:]
        upper = (me & step) != 0
        send = jnp.where(upper, low, high)
        keep = jnp.where(upper, high, low)
        got = lax.ppermute(send, axis, [(i, i ^ step) for i in range(size)])
        x = keep + got
        step = step * 2
    return x


def gather_back(x, axis):
    size = lax.axis_size(axis)
    me = lax.axis_index(axis)
    step = size // 2
    while step:
        got = lax.ppermute(x, axis, [(i, i ^ step) for i in range(size)])
        upper = (me & step) != 0
        x = jnp.concatenate([jnp.where(upper, got, x), jnp.where(upper, x, got)], axis=-2)
        step = step // 2
    return x


def coeff_kernel(rows, features, gram_ref, down_ref, across_ref, j0_ref, j1_ref, d0_ref, d1_ref):
    span = j0_ref.shape[0]
    batch = gram_ref.shape[0] - span
    rest = span - rows
    inverse_square = 1.0 / features / features
    rhs = ((1,), (1,))

    def coefficients(left, right, first):
        corr = dot(left, right, rhs, HIGH) * inverse_square
        down, across = down_ref[first:, :], across_ref[...]
        mixing = jnp.where(across < down, -through_bf16(corr), 0.0)
        mixing = jnp.where(across == down, 1.0, mixing)
        return through_bf16(left / features), mixing

    def scale(left, product):
        norm = jnp.maximum(jnp.sum(left * product, axis=1, keepdims=True), 0.0)
        return jnp.sqrt(features / (norm + 1e-06))

    proj = gram_ref[batch:, :batch]
    reward, mixing = coefficients(proj, proj, 0)
    j0 = jnp.concatenate([reward, mixing], axis=1)
    y0 = dot(j0, gram_ref[...], precision=HIGH)
    d0 = scale(j0, y0)
    j0_ref[...] = j0.astype(jnp.bfloat16)
    d0_ref[...] = d0
    proj1 = d0 * y0[:, :batch]
    reward, mixing = coefficients(proj1[rest:], proj1, rest)
    j1_ref[:, :batch] = reward.astype(jnp.bfloat16)
    j1_ref[:, batch:] = mixing.astype(jnp.bfloat16)
    joint = dot(mixing, d0 * j0, precision=HIGH)
    joint = jnp.concatenate([joint[:, :batch] + reward, joint[:, batch:]], axis=1)
    d1_ref[...] = scale(joint, dot(joint, gram_ref[...], precision=HIGH))


def coefficients_of(gram, order, rows, features):
    span = order.shape[0]
    size = gram.shape[0]
    return pl.pallas_call(
        functools.partial(coeff_kernel, rows, features),
        out_shape=[
            jax.ShapeDtypeStruct((span, size), jnp.bfloat16),
            jax.ShapeDtypeStruct((rows, size), jnp.bfloat16),
            jax.ShapeDtypeStruct((span, 1), jnp.float32),
            jax.ShapeDtypeStruct((rows, 1), jnp.float32),
        ],
        cost_estimate=pl.CostEstimate(
            flops=24 * size * size * span, bytes_accessed=8 * size * size, transcendentals=0
        ),
        name="coefficients_of",
    )(gram, order[:, None], order[None, :])


def update_kernel(others, base_ref, w_ref, x_ref, *refs):
    other_refs = refs[:others]
    j0_ref, j1_ref, d0_ref, d1_ref = refs[others : others + 4]
    out_ref, stack, scaled = refs[-3:]
    rows, batch = w_ref.shape[0], x_ref.shape[0]
    rest = others * rows
    split = batch + rest
    stack[:batch, :] = x_ref[...]
    scaled[:batch, :] = x_ref[...]
    for i in range(others):
        stack[batch + i * rows : batch + (i + 1) * rows, :] = other_refs[i][...]
    stack[split:, :] = w_ref[...]
    first = dot(j0_ref[:rest, :split], stack[:split, :])
    scaled[batch:split, :] = (first * d0_ref[:rest, :]).astype(jnp.bfloat16)
    own = dot(j0_ref[rest:, :], stack[...])
    scaled[split:, :] = (own * d0_ref[rest:, :]).astype(jnp.bfloat16)
    out_ref[...] = (dot(j1_ref[...], scaled[...]) * d1_ref[...]).astype(jnp.bfloat16)


def update_piece(base, weights, slab, others, coeffs, out, width, block):
    rows, batch = weights.shape[0], slab.shape[0]
    count = len(others)
    shift = lambda i, b: (0, b[0] + i)
    whole = lambda i, b: (0, 0)
    in_specs = [pl.BlockSpec((rows, block), shift), pl.BlockSpec((batch, block), shift)]
    in_specs += [pl.BlockSpec((rows, block), lambda i, b: (0, i))] * count
    in_specs += [pl.BlockSpec(c.shape, whole) for c in coeffs]
    operands = [weights, slab, *others, *coeffs]
    aliases = {}
    if out is not None:
        in_specs.append(pl.BlockSpec(memory_space=pl.ANY))
        operands.append(out)
        aliases = {len(operands): 0}
    total = rows * (count + 1)
    return pl.pallas_call(
        functools.partial(update_kernel, count),
        out_shape=jax.ShapeDtypeStruct(weights.shape, jnp.bfloat16),
        grid_spec=pltpu.PrefetchScalarGridSpec(
            num_scalar_prefetch=1,
            grid=(width // block,),
            in_specs=in_specs,
            out_specs=pl.BlockSpec((rows, block), shift),
            scratch_shapes=[
                pltpu.VMEM((total + batch, block), jnp.bfloat16),
                pltpu.VMEM((total + batch, block), jnp.bfloat16),
            ],
        ),
        input_output_aliases=aliases,
        compiler_params=pltpu.CompilerParams(dimension_semantics=("arbitrary",)),
        cost_estimate=pl.CostEstimate(
            flops=2 * width * (total + batch) * (total + rows),
            bytes_accessed=2 * width * (2 * rows + batch + count * rows),
            transcendentals=0,
        ),
        name="update_piece",
    )(base, *operands)


def compute(slab, players):
    rows, width = players.shape
    batch = slab.shape[0]
    n = lax.axis_size("player")
    me = lax.axis_index("player")
    features = width * lax.axis_size("feat")
    half, unit = width // 2, width // UNIT
    ring = [[(i, (i + s) % n) for i in range(n)] for s in range(n)]

    sent_at = [jnp.where(me + s < n, 0, half) for s in range(n)]
    got_at = [jnp.where(me - s >= 0, 0, half) for s in range(n)]

    source = players

    def send(s, start, size):
        nonlocal source
        piece = lax.dynamic_slice(source, (0, start), (rows, size))
        source, piece = lax.optimization_barrier((source, piece))
        return lax.ppermute(piece, "player", ring[s])

    early, late, place = [], [], 0
    for units in EARLY:
        size = units * unit
        early.append((place, size, [send(s, sent_at[s] + place, size) for s in range(1, n)]))
        place += size
    place = 0
    for units in LATE:
        size = units * unit
        late.append(
            (
                place,
                size,
                [send(s, half - sent_at[s] + place, size) for s in range(1, n)],
            )
        )
        place += size

    rhs = ((1,), (1,))
    own_gram = dot(source, source, rhs)
    own_proj = dot(source, slab, rhs)
    slab_gram = dot(slab, slab, rhs)
    cross = []
    for s in range(1, n):
        total = 0.0
        for place, size, got in early:
            mine = lax.dynamic_slice(players, (0, got_at[s] + place), (rows, size))
            piece = got[s - 1]
            if place:
                total, piece = lax.optimization_barrier((total, piece))
            total = total + dot(mine, piece, rhs)
        cross.append(total)

    if batch >= rows:
        flat = [slab_gram[i : i + rows] for i in range(0, batch, rows)]
    else:
        flat = [jnp.pad(slab_gram, ((0, rows - batch), (0, 0)))]
    payload = jnp.concatenate([own_gram, *cross, own_proj, *flat], axis=1)
    part = scatter_sum(payload, "feat")
    parts = [part] + [lax.ppermute(part, "player", ring[s]) for s in range(1, n)]
    full = gather_back(jnp.stack(parts), "feat")

    span = n * rows
    turn = [*range(1, n), 0]
    block_of = lambda t, u: full[t, :, ((u - t) % n) * rows : ((u - t) % n + 1) * rows]
    pair = lambda t, u: block_of(t, u) if t == u else block_of(t, u) + block_of(u, t).T
    proj = jnp.concatenate([full[t, :, span : span + batch] for t in turn], axis=0)
    tail = full[0, :, span + batch :]
    if batch >= rows:
        hmat = jnp.concatenate(
            [tail[:, i * batch : (i + 1) * batch] for i in range(batch // rows)], axis=0
        )
    else:
        hmat = tail[:batch]
    lines = [jnp.concatenate([hmat, proj.T], axis=1)]
    for k, t in enumerate(turn):
        left = proj[k * rows : (k + 1) * rows]
        lines.append(jnp.concatenate([left, *[pair(t, u) for u in turn]], axis=1))
    gram = jnp.concatenate(lines, axis=0)
    order = jnp.concatenate(
        [((me - t) % n) * rows + jnp.arange(rows, dtype=jnp.int32) for t in turn]
    )
    coeffs = coefficients_of(gram, order, rows, features)

    block = min(BLOCK, unit)
    first = jnp.where(me > 0, 0, half)
    out = None
    for start, pieces in ((first, early), (half - first, late)):
        for place, size, got in pieces:
            base = ((start + place) // block).reshape(1).astype(jnp.int32)
            out = update_piece(base, players, slab, got, coeffs, out, size, block)
    return out


def solution(mesh):
    in_specs = (P(None, "feat"), P("player", "feat"))
    out_specs = P("player", "feat")
    return jax.shard_map(
        compute, mesh=mesh, in_specs=in_specs, out_specs=out_specs, check_vma=False
    )
```

```python
import functools

import jax
import jax.numpy as jnp
from jax import lax
from jax.experimental import pallas as pl
from jax.experimental.pallas import tpu as pltpu
from jax.sharding import PartitionSpec as P


EARLY = (1, 7, 24)
LATE = (6, 20, 4, 1, 1)
UNIT = 64
BLOCKS = (1024, 512, 256, 128)


HIGH = lax.Precision.HIGHEST


def dot(a, b, contract=((1,), (0,)), precision=None):
    return lax.dot_general(
        a, b, (contract, ((), ())), precision=precision, preferred_element_type=jnp.float32
    )


def through_bf16(x):
    return x.astype(jnp.bfloat16).astype(jnp.float32)


def scatter_sum(x, axis):
    size = lax.axis_size(axis)
    me = lax.axis_index(axis)
    step = 1
    while step < size:
        half = x.shape[0] // 2
        low, high = x[:half], x[half:]
        upper = (me & step) != 0
        send = jnp.where(upper, low, high)
        keep = jnp.where(upper, high, low)
        got = lax.ppermute(send, axis, [(i, i ^ step) for i in range(size)])
        x = keep + got
        step = step * 2
    return x


def gather_back(x, axis):
    size = lax.axis_size(axis)
    me = lax.axis_index(axis)
    step = size // 2
    while step:
        got = lax.ppermute(x, axis, [(i, i ^ step) for i in range(size)])
        upper = (me & step) != 0
        x = jnp.concatenate([jnp.where(upper, got, x), jnp.where(upper, x, got)], axis=-2)
        step = step // 2
    return x


def coeff_kernel(rows, features, gram_ref, down_ref, across_ref, j0_ref, j1_ref, d0_ref, d1_ref):
    span = j0_ref.shape[0]
    batch = gram_ref.shape[0] - span
    rest = span - rows
    inverse_square = 1.0 / features / features
    rhs = ((1,), (1,))

    def coefficients(left, right, first):
        corr = dot(left, right, rhs, HIGH) * inverse_square
        down, across = down_ref[first:, :], across_ref[...]
        mixing = jnp.where(across < down, -through_bf16(corr), 0.0)
        mixing = jnp.where(across == down, 1.0, mixing)
        return through_bf16(left / features), mixing

    def scale(left, product):
        norm = jnp.maximum(jnp.sum(left * product, axis=1, keepdims=True), 0.0)
        return jnp.sqrt(features / (norm + 1e-06))

    proj = gram_ref[batch:, :batch]
    reward, mixing = coefficients(proj, proj, 0)
    j0 = jnp.concatenate([reward, mixing], axis=1)
    y0 = dot(j0, gram_ref[...], precision=HIGH)
    d0 = scale(j0, y0)
    j0_ref[...] = j0.astype(jnp.bfloat16)
    d0_ref[...] = d0
    proj1 = d0 * y0[:, :batch]
    reward, mixing = coefficients(proj1[rest:], proj1, rest)
    j1_ref[:, :batch] = reward.astype(jnp.bfloat16)
    j1_ref[:, batch:] = mixing.astype(jnp.bfloat16)
    joint = dot(mixing, d0 * j0, precision=HIGH)
    joint = jnp.concatenate([joint[:, :batch] + reward, joint[:, batch:]], axis=1)
    d1_ref[...] = scale(joint, dot(joint, gram_ref[...], precision=HIGH))


def coefficients_of(gram, order, rows, features):
    span = order.shape[0]
    size = gram.shape[0]
    return pl.pallas_call(
        functools.partial(coeff_kernel, rows, features),
        out_shape=[
            jax.ShapeDtypeStruct((span, size), jnp.bfloat16),
            jax.ShapeDtypeStruct((rows, size), jnp.bfloat16),
            jax.ShapeDtypeStruct((span, 1), jnp.float32),
            jax.ShapeDtypeStruct((rows, 1), jnp.float32),
        ],
        cost_estimate=pl.CostEstimate(
            flops=24 * size * size * span, bytes_accessed=8 * size * size, transcendentals=0
        ),
        name="coefficients_of",
    )(gram, order[:, None], order[None, :])


def update_kernel(others, base_ref, w_ref, x_ref, *refs):
    other_refs = refs[:others]
    j0_ref, j1_ref, d0_ref, d1_ref = refs[others : others + 4]
    out_ref, stack, scaled = refs[-3:]
    rows, batch = w_ref.shape[0], x_ref.shape[0]
    rest = others * rows
    split = batch + rest
    stack[:batch, :] = x_ref[...]
    scaled[:batch, :] = x_ref[...]
    for i in range(others):
        stack[batch + i * rows : batch + (i + 1) * rows, :] = other_refs[i][...]
    stack[split:, :] = w_ref[...]
    first = dot(j0_ref[:rest, :split], stack[:split, :])
    scaled[batch:split, :] = (first * d0_ref[:rest, :]).astype(jnp.bfloat16)
    own = dot(j0_ref[rest:, :], stack[...])
    scaled[split:, :] = (own * d0_ref[rest:, :]).astype(jnp.bfloat16)
    out_ref[...] = (dot(j1_ref[...], scaled[...]) * d1_ref[...]).astype(jnp.bfloat16)


def update_piece(base, weights, slab, others, coeffs, out, width, block):
    rows, batch = weights.shape[0], slab.shape[0]
    count = len(others)
    shift = lambda i, b: (0, b[0] + i)
    whole = lambda i, b: (0, 0)
    in_specs = [pl.BlockSpec((rows, block), shift), pl.BlockSpec((batch, block), shift)]
    in_specs += [pl.BlockSpec((rows, block), lambda i, b: (0, i))] * count
    in_specs += [pl.BlockSpec(c.shape, whole) for c in coeffs]
    operands = [weights, slab, *others, *coeffs]
    aliases = {}
    if out is not None:
        in_specs.append(pl.BlockSpec(memory_space=pl.ANY))
        operands.append(out)
        aliases = {len(operands): 0}
    total = rows * (count + 1)
    return pl.pallas_call(
        functools.partial(update_kernel, count),
        out_shape=jax.ShapeDtypeStruct(weights.shape, jnp.bfloat16),
        grid_spec=pltpu.PrefetchScalarGridSpec(
            num_scalar_prefetch=1,
            grid=(width // block,),
            in_specs=in_specs,
            out_specs=pl.BlockSpec((rows, block), shift),
            scratch_shapes=[
                pltpu.VMEM((total + batch, block), jnp.bfloat16),
                pltpu.VMEM((total + batch, block), jnp.bfloat16),
            ],
        ),
        input_output_aliases=aliases,
        compiler_params=pltpu.CompilerParams(dimension_semantics=("arbitrary",)),
        cost_estimate=pl.CostEstimate(
            flops=2 * width * (total + batch) * (total + rows),
            bytes_accessed=2 * width * (2 * rows + batch + count * rows),
            transcendentals=0,
        ),
        name="update_piece",
    )(base, *operands)


def compute(slab, players):
    rows, width = players.shape
    batch = slab.shape[0]
    n = lax.axis_size("player")
    me = lax.axis_index("player")
    features = width * lax.axis_size("feat")
    half, unit = width // 2, width // UNIT
    ring = [[(i, (i + s) % n) for i in range(n)] for s in range(n)]

    sent_at = [jnp.where(me + s < n, 0, half) for s in range(n)]
    got_at = [jnp.where(me - s >= 0, 0, half) for s in range(n)]

    source = players

    def send(s, start, size):
        nonlocal source
        piece = lax.dynamic_slice(source, (0, start), (rows, size))
        source, piece = lax.optimization_barrier((source, piece))
        return lax.ppermute(piece, "player", ring[s])

    early, late, place = [], [], 0
    for units in EARLY:
        size = units * unit
        early.append((place, size, [send(s, sent_at[s] + place, size) for s in range(1, n)]))
        place += size
    place = 0
    for units in LATE:
        size = units * unit
        late.append(
            (
                place,
                size,
                [send(s, half - sent_at[s] + place, size) for s in range(1, n)],
            )
        )
        place += size

    rhs = ((1,), (1,))
    own_gram = dot(source, source, rhs)
    own_proj = dot(source, slab, rhs)
    slab_gram = dot(slab, slab, rhs)
    cross = []
    for s in range(1, n):
        total = 0.0
        for place, size, got in early:
            mine = lax.dynamic_slice(players, (0, got_at[s] + place), (rows, size))
            piece = got[s - 1]
            if place:
                total, piece = lax.optimization_barrier((total, piece))
            total = total + dot(mine, piece, rhs)
        cross.append(total)

    if batch >= rows:
        flat = [slab_gram[i : i + rows] for i in range(0, batch, rows)]
    else:
        flat = [jnp.pad(slab_gram, ((0, rows - batch), (0, 0)))]
    payload = jnp.concatenate([own_gram, *cross, own_proj, *flat], axis=1)
    part = scatter_sum(payload, "feat")
    parts = [part] + [lax.ppermute(part, "player", ring[s]) for s in range(1, n)]
    full = gather_back(jnp.stack(parts), "feat")

    span = n * rows
    turn = [*range(1, n), 0]
    block_of = lambda t, u: full[t, :, ((u - t) % n) * rows : ((u - t) % n + 1) * rows]
    pair = lambda t, u: block_of(t, u) if t == u else block_of(t, u) + block_of(u, t).T
    proj = jnp.concatenate([full[t, :, span : span + batch] for t in turn], axis=0)
    tail = full[0, :, span + batch :]
    if batch >= rows:
        hmat = jnp.concatenate(
            [tail[:, i * batch : (i + 1) * batch] for i in range(batch // rows)], axis=0
        )
    else:
        hmat = tail[:batch]
    lines = [jnp.concatenate([hmat, proj.T], axis=1)]
    for k, t in enumerate(turn):
        left = proj[k * rows : (k + 1) * rows]
        lines.append(jnp.concatenate([left, *[pair(t, u) for u in turn]], axis=1))
    gram = jnp.concatenate(lines, axis=0)
    order = jnp.concatenate(
        [((me - t) % n) * rows + jnp.arange(rows, dtype=jnp.int32) for t in turn]
    )
    coeffs = coefficients_of(gram, order, rows, features)

    first = jnp.where(me > 0, 0, half)
    out = None
    for start, pieces in ((first, early), (half - first, late)):
        for place, size, got in pieces:
            block = next(b for b in BLOCKS if size % b == 0 and place % b == 0)
            base = ((start + place) // block).reshape(1).astype(jnp.int32)
            out = update_piece(base, players, slab, got, coeffs, out, size, block)
    return out


def solution(mesh):
    in_specs = (P(None, "feat"), P("player", "feat"))
    out_specs = P("player", "feat")
    return jax.shard_map(
        compute, mesh=mesh, in_specs=in_specs, out_specs=out_specs, check_vma=False
    )
```

```python
import functools

import jax
import jax.numpy as jnp
from jax import lax
from jax.experimental import pallas as pl
from jax.experimental.pallas import tpu as pltpu
from jax.sharding import PartitionSpec as P


EARLY = (1, 7, 24)
LATE = (6, 20, 4, 1, 1)
NEAR = 1
UNIT = 64
BLOCKS = (1024, 512, 256, 128)


HIGH = lax.Precision.HIGHEST


def dot(a, b, contract=((1,), (0,)), precision=None):
    return lax.dot_general(
        a, b, (contract, ((), ())), precision=precision, preferred_element_type=jnp.float32
    )


def through_bf16(x):
    return x.astype(jnp.bfloat16).astype(jnp.float32)


def scatter_sum(x, axis):
    size = lax.axis_size(axis)
    me = lax.axis_index(axis)
    step = 1
    while step < size:
        half = x.shape[0] // 2
        low, high = x[:half], x[half:]
        upper = (me & step) != 0
        send = jnp.where(upper, low, high)
        keep = jnp.where(upper, high, low)
        got = lax.ppermute(send, axis, [(i, i ^ step) for i in range(size)])
        x = keep + got
        step = step * 2
    return x


def gather_back(x, axis):
    size = lax.axis_size(axis)
    me = lax.axis_index(axis)
    step = size // 2
    while step:
        got = lax.ppermute(x, axis, [(i, i ^ step) for i in range(size)])
        upper = (me & step) != 0
        x = jnp.concatenate([jnp.where(upper, got, x), jnp.where(upper, x, got)], axis=-2)
        step = step // 2
    return x


def coeff_kernel(rows, features, gram_ref, down_ref, across_ref, j0_ref, j1_ref, d0_ref, d1_ref):
    span = j0_ref.shape[0]
    batch = gram_ref.shape[0] - span
    rest = span - rows
    inverse_square = 1.0 / features / features
    rhs = ((1,), (1,))

    def coefficients(left, right, first):
        corr = dot(left, right, rhs, HIGH) * inverse_square
        down, across = down_ref[first:, :], across_ref[...]
        mixing = jnp.where(across < down, -through_bf16(corr), 0.0)
        mixing = jnp.where(across == down, 1.0, mixing)
        return through_bf16(left / features), mixing

    def scale(left, product):
        norm = jnp.maximum(jnp.sum(left * product, axis=1, keepdims=True), 0.0)
        return jnp.sqrt(features / (norm + 1e-06))

    proj = gram_ref[batch:, :batch]
    reward, mixing = coefficients(proj, proj, 0)
    j0 = jnp.concatenate([reward, mixing], axis=1)
    y0 = dot(j0, gram_ref[...], precision=HIGH)
    d0 = scale(j0, y0)
    j0_ref[...] = j0.astype(jnp.bfloat16)
    d0_ref[...] = d0
    proj1 = d0 * y0[:, :batch]
    reward, mixing = coefficients(proj1[rest:], proj1, rest)
    j1_ref[:, :batch] = reward.astype(jnp.bfloat16)
    j1_ref[:, batch:] = mixing.astype(jnp.bfloat16)
    joint = dot(mixing, d0 * j0, precision=HIGH)
    joint = jnp.concatenate([joint[:, :batch] + reward, joint[:, batch:]], axis=1)
    d1_ref[...] = scale(joint, dot(joint, gram_ref[...], precision=HIGH))


def coefficients_of(gram, order, rows, features):
    span = order.shape[0]
    size = gram.shape[0]
    return pl.pallas_call(
        functools.partial(coeff_kernel, rows, features),
        out_shape=[
            jax.ShapeDtypeStruct((span, size), jnp.bfloat16),
            jax.ShapeDtypeStruct((rows, size), jnp.bfloat16),
            jax.ShapeDtypeStruct((span, 1), jnp.float32),
            jax.ShapeDtypeStruct((rows, 1), jnp.float32),
        ],
        cost_estimate=pl.CostEstimate(
            flops=24 * size * size * span, bytes_accessed=8 * size * size, transcendentals=0
        ),
        name="coefficients_of",
    )(gram, order[:, None], order[None, :])


def update_kernel(others, base_ref, w_ref, x_ref, *refs):
    other_refs = refs[:others]
    j0_ref, j1_ref, d0_ref, d1_ref = refs[others : others + 4]
    out_ref, stack, scaled = refs[-3:]
    rows, batch = w_ref.shape[0], x_ref.shape[0]
    rest = others * rows
    split = batch + rest
    stack[:batch, :] = x_ref[...]
    scaled[:batch, :] = x_ref[...]
    for i in range(others):
        stack[batch + i * rows : batch + (i + 1) * rows, :] = other_refs[i][...]
    stack[split:, :] = w_ref[...]
    first = dot(j0_ref[:rest, :split], stack[:split, :])
    scaled[batch:split, :] = (first * d0_ref[:rest, :]).astype(jnp.bfloat16)
    own = dot(j0_ref[rest:, :], stack[...])
    scaled[split:, :] = (own * d0_ref[rest:, :]).astype(jnp.bfloat16)
    out_ref[...] = (dot(j1_ref[...], scaled[...]) * d1_ref[...]).astype(jnp.bfloat16)


def update_piece(base, weights, slab, others, coeffs, out, width, block, near):
    rows, batch = weights.shape[0], slab.shape[0]
    count = len(others)
    shift = lambda i, b: (0, b[0] + i)
    in_specs = [pl.BlockSpec((rows, block), shift), pl.BlockSpec((batch, block), shift)]
    in_specs += [pl.BlockSpec((rows, block), lambda i, b: (0, i))] * count
    if near:
        cut = lambda x: lax.dynamic_slice(x, (0, base[0] * block), (x.shape[0], block))
        inputs = [cut(weights), cut(slab), *others]
        inputs = [pltpu.with_memory_space_constraint(x, pltpu.VMEM) for x in inputs]
        in_specs = [pl.BlockSpec(memory_space=pltpu.VMEM)] * len(inputs)
    else:
        inputs = [weights, slab, *others]
    in_specs += [pl.BlockSpec(memory_space=pltpu.VMEM)] * len(coeffs)
    operands = [*inputs, *coeffs]
    aliases = {}
    if out is not None:
        in_specs.append(pl.BlockSpec(memory_space=pl.ANY))
        operands.append(out)
        aliases = {len(operands): 0}
    total = rows * (count + 1)
    return pl.pallas_call(
        functools.partial(update_kernel, count),
        out_shape=jax.ShapeDtypeStruct(weights.shape, jnp.bfloat16),
        grid_spec=pltpu.PrefetchScalarGridSpec(
            num_scalar_prefetch=1,
            grid=(width // block,),
            in_specs=in_specs,
            out_specs=pl.BlockSpec((rows, block), shift),
            scratch_shapes=[
                pltpu.VMEM((total + batch, block), jnp.bfloat16),
                pltpu.VMEM((total + batch, block), jnp.bfloat16),
            ],
        ),
        input_output_aliases=aliases,
        compiler_params=pltpu.CompilerParams(dimension_semantics=("arbitrary",)),
        cost_estimate=pl.CostEstimate(
            flops=2 * width * (total + batch) * (total + rows),
            bytes_accessed=2 * width * (2 * rows + batch + count * rows),
            transcendentals=0,
        ),
        name="update_piece",
    )(base, *operands)


def compute(slab, players):
    rows, width = players.shape
    batch = slab.shape[0]
    n = lax.axis_size("player")
    me = lax.axis_index("player")
    features = width * lax.axis_size("feat")
    half, unit = width // 2, width // UNIT
    ring = [[(i, (i + s) % n) for i in range(n)] for s in range(n)]

    sent_at = [jnp.where(me + s < n, 0, half) for s in range(n)]
    got_at = [jnp.where(me - s >= 0, 0, half) for s in range(n)]

    source = players

    def send(s, start, size):
        nonlocal source
        piece = lax.dynamic_slice(source, (0, start), (rows, size))
        source, piece = lax.optimization_barrier((source, piece))
        return lax.ppermute(piece, "player", ring[s])

    early, late, place = [], [], 0
    for units in EARLY:
        size = units * unit
        early.append((place, size, [send(s, sent_at[s] + place, size) for s in range(1, n)]))
        place += size
    place = 0
    for units in LATE:
        size = units * unit
        late.append(
            (
                place,
                size,
                [send(s, half - sent_at[s] + place, size) for s in range(1, n)],
            )
        )
        place += size

    rhs = ((1,), (1,))
    own_gram = dot(source, source, rhs)
    own_proj = dot(source, slab, rhs)
    slab_gram = dot(slab, slab, rhs)
    cross = []
    for s in range(1, n):
        total = 0.0
        for place, size, got in early:
            mine = lax.dynamic_slice(players, (0, got_at[s] + place), (rows, size))
            piece = got[s - 1]
            if place:
                total, piece = lax.optimization_barrier((total, piece))
            total = total + dot(mine, piece, rhs)
        cross.append(total)

    if batch >= rows:
        flat = [slab_gram[i : i + rows] for i in range(0, batch, rows)]
    else:
        flat = [jnp.pad(slab_gram, ((0, rows - batch), (0, 0)))]
    payload = jnp.concatenate([own_gram, *cross, own_proj, *flat], axis=1)
    part = scatter_sum(payload, "feat")
    parts = [part] + [lax.ppermute(part, "player", ring[s]) for s in range(1, n)]
    full = gather_back(jnp.stack(parts), "feat")

    span = n * rows
    turn = [*range(1, n), 0]
    block_of = lambda t, u: full[t, :, ((u - t) % n) * rows : ((u - t) % n + 1) * rows]
    pair = lambda t, u: block_of(t, u) if t == u else block_of(t, u) + block_of(u, t).T
    proj = jnp.concatenate([full[t, :, span : span + batch] for t in turn], axis=0)
    tail = full[0, :, span + batch :]
    if batch >= rows:
        hmat = jnp.concatenate(
            [tail[:, i * batch : (i + 1) * batch] for i in range(batch // rows)], axis=0
        )
    else:
        hmat = tail[:batch]
    lines = [jnp.concatenate([hmat, proj.T], axis=1)]
    for k, t in enumerate(turn):
        left = proj[k * rows : (k + 1) * rows]
        lines.append(jnp.concatenate([left, *[pair(t, u) for u in turn]], axis=1))
    gram = jnp.concatenate(lines, axis=0)
    order = jnp.concatenate(
        [((me - t) % n) * rows + jnp.arange(rows, dtype=jnp.int32) for t in turn]
    )
    coeffs = coefficients_of(gram, order, rows, features)
    coeffs = [pltpu.with_memory_space_constraint(c, pltpu.VMEM) for c in coeffs]

    first = jnp.where(me > 0, 0, half)
    out = None
    for name, start, pieces in (("e", first, early), ("l", half - first, late)):
        for k, (place, size, got) in enumerate(pieces):
            block = next(b for b in BLOCKS if size % b == 0 and place % b == 0)
            base = ((start + place) // block).reshape(1).astype(jnp.int32)
            near = name == "l" and size == block and k >= len(LATE) - NEAR
            out = update_piece(base, players, slab, got, coeffs, out, size, block, near)
    return out


def solution(mesh):
    in_specs = (P(None, "feat"), P("player", "feat"))
    out_specs = P("player", "feat")
    return jax.shard_map(
        compute, mesh=mesh, in_specs=in_specs, out_specs=out_specs, check_vma=False
    )
```

```python
import functools

import jax
import jax.numpy as jnp
from jax import lax
from jax.experimental import pallas as pl
from jax.experimental.pallas import tpu as pltpu
from jax.sharding import PartitionSpec as P


EARLY = (1, 7, 24)
LATE = (6, 20, 4, 1, 1)
NEAR = 2
UNIT = 64
BLOCKS = (1024, 512, 256, 128)


HIGH = lax.Precision.HIGHEST


def dot(a, b, contract=((1,), (0,)), precision=None):
    return lax.dot_general(
        a, b, (contract, ((), ())), precision=precision, preferred_element_type=jnp.float32
    )


def through_bf16(x):
    return x.astype(jnp.bfloat16).astype(jnp.float32)


def scatter_sum(x, axis):
    size = lax.axis_size(axis)
    me = lax.axis_index(axis)
    step = 1
    while step < size:
        half = x.shape[0] // 2
        low, high = x[:half], x[half:]
        upper = (me & step) != 0
        send = jnp.where(upper, low, high)
        keep = jnp.where(upper, high, low)
        got = lax.ppermute(send, axis, [(i, i ^ step) for i in range(size)])
        x = keep + got
        step = step * 2
    return x


def gather_back(x, axis):
    size = lax.axis_size(axis)
    me = lax.axis_index(axis)
    step = size // 2
    while step:
        got = lax.ppermute(x, axis, [(i, i ^ step) for i in range(size)])
        upper = (me & step) != 0
        x = jnp.concatenate([jnp.where(upper, got, x), jnp.where(upper, x, got)], axis=-2)
        step = step // 2
    return x


def coeff_kernel(rows, features, gram_ref, down_ref, across_ref, j0_ref, j1_ref, d0_ref, d1_ref):
    span = j0_ref.shape[0]
    batch = gram_ref.shape[0] - span
    rest = span - rows
    inverse_square = 1.0 / features / features
    rhs = ((1,), (1,))

    def coefficients(left, right, first):
        corr = dot(left, right, rhs, HIGH) * inverse_square
        down, across = down_ref[first:, :], across_ref[...]
        mixing = jnp.where(across < down, -through_bf16(corr), 0.0)
        mixing = jnp.where(across == down, 1.0, mixing)
        return through_bf16(left / features), mixing

    def scale(left, product):
        norm = jnp.maximum(jnp.sum(left * product, axis=1, keepdims=True), 0.0)
        return jnp.sqrt(features / (norm + 1e-06))

    proj = gram_ref[batch:, :batch]
    reward, mixing = coefficients(proj, proj, 0)
    j0 = jnp.concatenate([reward, mixing], axis=1)
    y0 = dot(j0, gram_ref[...], precision=HIGH)
    d0 = scale(j0, y0)
    j0_ref[...] = j0.astype(jnp.bfloat16)
    d0_ref[...] = d0
    proj1 = d0 * y0[:, :batch]
    reward, mixing = coefficients(proj1[rest:], proj1, rest)
    j1_ref[:, :batch] = reward.astype(jnp.bfloat16)
    j1_ref[:, batch:] = mixing.astype(jnp.bfloat16)
    joint = dot(mixing, d0 * j0, precision=HIGH)
    joint = jnp.concatenate([joint[:, :batch] + reward, joint[:, batch:]], axis=1)
    d1_ref[...] = scale(joint, dot(joint, gram_ref[...], precision=HIGH))


def coefficients_of(gram, order, rows, features):
    span = order.shape[0]
    size = gram.shape[0]
    return pl.pallas_call(
        functools.partial(coeff_kernel, rows, features),
        out_shape=[
            jax.ShapeDtypeStruct((span, size), jnp.bfloat16),
            jax.ShapeDtypeStruct((rows, size), jnp.bfloat16),
            jax.ShapeDtypeStruct((span, 1), jnp.float32),
            jax.ShapeDtypeStruct((rows, 1), jnp.float32),
        ],
        cost_estimate=pl.CostEstimate(
            flops=24 * size * size * span, bytes_accessed=8 * size * size, transcendentals=0
        ),
        name="coefficients_of",
    )(gram, order[:, None], order[None, :])


def update_kernel(others, base_ref, w_ref, x_ref, *refs):
    other_refs = refs[:others]
    j0_ref, j1_ref, d0_ref, d1_ref = refs[others : others + 4]
    out_ref, stack, scaled = refs[-3:]
    rows, batch = w_ref.shape[0], x_ref.shape[0]
    rest = others * rows
    split = batch + rest
    stack[:batch, :] = x_ref[...]
    scaled[:batch, :] = x_ref[...]
    for i in range(others):
        stack[batch + i * rows : batch + (i + 1) * rows, :] = other_refs[i][...]
    stack[split:, :] = w_ref[...]
    first = dot(j0_ref[:rest, :split], stack[:split, :])
    scaled[batch:split, :] = (first * d0_ref[:rest, :]).astype(jnp.bfloat16)
    own = dot(j0_ref[rest:, :], stack[...])
    scaled[split:, :] = (own * d0_ref[rest:, :]).astype(jnp.bfloat16)
    out_ref[...] = (dot(j1_ref[...], scaled[...]) * d1_ref[...]).astype(jnp.bfloat16)


def update_piece(base, weights, slab, others, coeffs, out, width, block, near):
    rows, batch = weights.shape[0], slab.shape[0]
    count = len(others)
    shift = lambda i, b: (0, b[0] + i)
    in_specs = [pl.BlockSpec((rows, block), shift), pl.BlockSpec((batch, block), shift)]
    in_specs += [pl.BlockSpec((rows, block), lambda i, b: (0, i))] * count
    if near:
        cut = lambda x: lax.dynamic_slice(x, (0, base[0] * block), (x.shape[0], block))
        inputs = [cut(weights), cut(slab), *others]
        inputs = [pltpu.with_memory_space_constraint(x, pltpu.VMEM) for x in inputs]
        in_specs = [pl.BlockSpec(memory_space=pltpu.VMEM)] * len(inputs)
    else:
        inputs = [weights, slab, *others]
    in_specs += [pl.BlockSpec(memory_space=pltpu.VMEM)] * len(coeffs)
    operands = [*inputs, *coeffs]
    aliases = {}
    if out is not None:
        in_specs.append(pl.BlockSpec(memory_space=pl.ANY))
        operands.append(out)
        aliases = {len(operands): 0}
    total = rows * (count + 1)
    return pl.pallas_call(
        functools.partial(update_kernel, count),
        out_shape=jax.ShapeDtypeStruct(weights.shape, jnp.bfloat16),
        grid_spec=pltpu.PrefetchScalarGridSpec(
            num_scalar_prefetch=1,
            grid=(width // block,),
            in_specs=in_specs,
            out_specs=pl.BlockSpec((rows, block), shift),
            scratch_shapes=[
                pltpu.VMEM((total + batch, block), jnp.bfloat16),
                pltpu.VMEM((total + batch, block), jnp.bfloat16),
            ],
        ),
        input_output_aliases=aliases,
        compiler_params=pltpu.CompilerParams(dimension_semantics=("arbitrary",)),
        cost_estimate=pl.CostEstimate(
            flops=2 * width * (total + batch) * (total + rows),
            bytes_accessed=2 * width * (2 * rows + batch + count * rows),
            transcendentals=0,
        ),
        name="update_piece",
    )(base, *operands)


def compute(slab, players):
    rows, width = players.shape
    batch = slab.shape[0]
    n = lax.axis_size("player")
    me = lax.axis_index("player")
    features = width * lax.axis_size("feat")
    half, unit = width // 2, width // UNIT
    late_sizes = [u * unit for u in LATE]
    late_sizes[-1:] = [late_sizes[-1] // 2] * 2 if unit >= 256 else late_sizes[-1:]
    ring = [[(i, (i + s) % n) for i in range(n)] for s in range(n)]

    sent_at = [jnp.where(me + s < n, 0, half) for s in range(n)]
    got_at = [jnp.where(me - s >= 0, 0, half) for s in range(n)]

    source = players

    onward = [[(i, i + s) for i in range(n - s)] for s in range(n)]

    def send(s, start, size, pairs):
        nonlocal source
        piece = lax.dynamic_slice(source, (0, start), (rows, size))
        source, piece = lax.optimization_barrier((source, piece))
        return lax.ppermute(piece, "player", pairs[s])

    early, late, place = [], [], 0
    for units in EARLY:
        size = units * unit
        early.append((place, size, [send(s, sent_at[s] + place, size, ring) for s in range(1, n)]))
        place += size
    place = 0
    for size in late_sizes:
        late.append(
            (
                place,
                size,
                [send(s, half - sent_at[s] + place, size, onward) for s in range(1, n)],
            )
        )
        place += size

    rhs = ((1,), (1,))
    own_gram = dot(source, source, rhs)
    own_proj = dot(source, slab, rhs)
    slab_gram = dot(slab, slab, rhs)
    cross = []
    for s in range(1, n):
        total = 0.0
        for place, size, got in early:
            mine = lax.dynamic_slice(players, (0, got_at[s] + place), (rows, size))
            piece = got[s - 1]
            if place:
                total, piece = lax.optimization_barrier((total, piece))
            total = total + dot(mine, piece, rhs)
        cross.append(total)

    if batch >= rows:
        flat = [slab_gram[i : i + rows] for i in range(0, batch, rows)]
    else:
        flat = [jnp.pad(slab_gram, ((0, rows - batch), (0, 0)))]
    payload = jnp.concatenate([own_gram, *cross, own_proj, *flat], axis=1)
    part = scatter_sum(payload, "feat")
    parts = [part] + [lax.ppermute(part, "player", ring[s]) for s in range(1, n)]
    full = gather_back(jnp.stack(parts), "feat")

    span = n * rows
    turn = [*range(1, n), 0]
    block_of = lambda t, u: full[t, :, ((u - t) % n) * rows : ((u - t) % n + 1) * rows]
    pair = lambda t, u: block_of(t, u) if t == u else block_of(t, u) + block_of(u, t).T
    proj = jnp.concatenate([full[t, :, span : span + batch] for t in turn], axis=0)
    tail = full[0, :, span + batch :]
    if batch >= rows:
        hmat = jnp.concatenate(
            [tail[:, i * batch : (i + 1) * batch] for i in range(batch // rows)], axis=0
        )
    else:
        hmat = tail[:batch]
    lines = [jnp.concatenate([hmat, proj.T], axis=1)]
    for k, t in enumerate(turn):
        left = proj[k * rows : (k + 1) * rows]
        lines.append(jnp.concatenate([left, *[pair(t, u) for u in turn]], axis=1))
    gram = jnp.concatenate(lines, axis=0)
    order = jnp.concatenate(
        [((me - t) % n) * rows + jnp.arange(rows, dtype=jnp.int32) for t in turn]
    )
    coeffs = coefficients_of(gram, order, rows, features)
    coeffs = [pltpu.with_memory_space_constraint(c, pltpu.VMEM) for c in coeffs]

    first = jnp.where(me > 0, 0, half)
    out = None
    for name, start, pieces in (("e", first, early), ("l", half - first, late)):
        for k, (place, size, got) in enumerate(pieces):
            block = next(b for b in BLOCKS if size % b == 0 and place % b == 0)
            base = ((start + place) // block).reshape(1).astype(jnp.int32)
            near = name == "l" and size == block and k >= len(late_sizes) - NEAR
            out = update_piece(base, players, slab, got, coeffs, out, size, block, near)
    return out


def solution(mesh):
    in_specs = (P(None, "feat"), P("player", "feat"))
    out_specs = P("player", "feat")
    return jax.shard_map(
        compute, mesh=mesh, in_specs=in_specs, out_specs=out_specs, check_vma=False
    )
```
